32 devices in a mesh: dp: 8 (over z, y), tensor: 4 (over x, core).
Axes of the slice: x: 2, y: 2, z: 4, core: 2. Of those that a mesh axis runs over, the one named last changes fastest.
Arguments:
- hidden_act: bfloat16 [8192, 7168], P('dp', 'tensor'), may hold values from -6 to 6
- out_grad: bfloat16 [8192, 4096], P(('dp', 'tensor')), may hold values from -3 to 3
- down_weight: bfloat16 [7168, 4096], P('tensor'), may hold values from -0.0625 to 0.0625
- kept_tiles: int32 [8, 52], P('dp', 'tensor'), may hold values from 0 to 447, as said below
- tile_owner: int32 [56, 32], P('tensor'), may hold values from 0 to 7, as said below
- moment1: float32 [8, 224, 16384], P('dp', 'tensor'), may hold values from -24 to 24
- moment2: float32 [8, 224, 16384], P('dp', 'tensor'), may hold values from 10 to 400
Outputs:
- grad_hidden: bfloat16 [8192, 7168], P('dp', 'tensor')
- moment1_new: float32 [8, 224, 16384], P('dp', 'tensor')
- moment2_new: float32 [8, 224, 16384], P('dp', 'tensor')
- weight_tiles: bfloat16 [8, 224, 16384], P('dp', 'tensor')
The draws below stay inside these ranges and needn't reach their ends.
Inputs may be any that keep to these rules, and one draw needn't show every extreme that they name: `kept_tiles`: within one device's 13 entries the tiles are distinct; they fall on ceil(13 / 3) different owners, 3 on each except the last; on every shard one owner receives 3 tiles from every replica. `tile_owner`: every owner owns exactly 56 tiles of every shard.
All inputs are finite; a program needn't handle non-finite values.
Results may differ from the reference program's by a relative error of at most 0.001.
Values may be sent and summed in bfloat16 or wider, within the bound.
A program may use at most 128 MiB of HBM per device.

```python
import math
import jax
import jax.numpy as jnp
from jax import lax

D = 4096
TILE = 128
TOK_DEV = 1024
STEP = 10
HID = 7168
TOKENS = 8192
BLK_ROWS = 14
BLK_COLS = 32
TILES_DEV = 448
OWN = 56
KEEP = 13
CAP = 3
N_DP = 8
N_TENSOR = 4


def owner_perm(key):
    base_key = jax.random.fold_in(key, 11)
    shard_keys = jax.random.split(base_key, N_TENSOR)
    return jax.vmap(lambda one_key: jax.random.permutation(one_key, TILES_DEV))(shard_keys).astype(jnp.int32)


def draw_tile_owner(key, part):
    perm = owner_perm(key)
    return (perm // OWN).astype(jnp.int32).reshape(N_TENSOR * BLK_ROWS, BLK_COLS)


def draw_kept_tiles(key, part):
    perm = owner_perm(key)
    inverse = jnp.argsort(perm, axis=1).astype(jnp.int32)
    pop_keys = jax.random.split(jax.random.fold_in(key, 23), N_TENSOR)
    popular = jax.vmap(lambda one_key: jax.random.permutation(one_key, N_DP))(pop_keys).astype(jnp.int32)
    noise = jax.random.randint(jax.random.fold_in(key, 37), (N_DP, N_TENSOR, N_DP), 0, N_DP).astype(jnp.int32)
    rank_pos = jnp.arange(N_DP, dtype=jnp.int32)
    score = (noise + rank_pos) * N_DP + rank_pos
    score = jnp.where(rank_pos == 0, -1, score)
    ordering = jnp.argsort(score, axis=-1).astype(jnp.int32)
    owners_seq = jnp.take_along_axis(jnp.broadcast_to(popular[None], (N_DP, N_TENSOR, N_DP)), ordering, axis=-1)
    picks = jnp.arange(KEEP, dtype=jnp.int32)
    group = picks // CAP
    pick_owner = owners_seq[:, :, group]
    starts = jax.random.randint(jax.random.fold_in(key, 41), (N_DP, N_TENSOR, N_DP), 0, OWN).astype(jnp.int32)
    pick_start = starts[:, :, group]
    position = (pick_start + picks % CAP) % OWN
    flat = pick_owner * OWN + position
    whole = jnp.broadcast_to(inverse[None], (N_DP, N_TENSOR, TILES_DEV))
    tiles = jnp.take_along_axis(whole, flat, axis=-1)
    return tiles.reshape(N_DP, N_TENSOR * KEEP).astype(jnp.int32)


def block_levels(own_key, dims, cuts, smallest, high):
    factor_of, own = 1.0, jax.random.fold_in(own_key, 6)
    for dim, parts in cuts:
        draws = jnp.exp(jax.random.uniform(jax.random.fold_in(own, dim), (parts,), jnp.float32, smallest / len(cuts), high / len(cuts)))
        factor_of = factor_of * jnp.repeat(draws, dims[dim] // parts).reshape([-1 if axis == dim else 1 for axis in range(len(dims))])
    return factor_of


def centred(rng, dims, scale, most, cuts=(), kind=jnp.bfloat16):
    level = block_levels(rng, dims, cuts, -0.22, 0.18) if cuts else 1.0
    result = jax.random.normal(rng, dims, jnp.float32) * scale * level
    return jnp.minimum(jnp.maximum(result, -most), most).astype(kind)


def setup_inputs(seed: int = 0) -> dict:
    key_of = jax.random.split(jax.random.key(seed), 8)
    hidden_act = centred(key_of[0], (TOKENS, HID), 1.0, 6.0, ((0, 8), (1, 4)))
    out_grad = centred(key_of[1], (TOKENS, D), 0.5, 3.0, ((0, 32),))
    down_weight = centred(key_of[2], (HID, D), HID ** -0.5, 0.0625, ((0, 4),))
    kept_tiles = draw_kept_tiles(jax.random.fold_in(key_of[7], 71), 0)
    tile_owner = draw_tile_owner(jax.random.fold_in(key_of[7], 71), 0)
    moment1 = centred(key_of[5], (N_DP, N_TENSOR * OWN, TILE * TILE), 4.0, 24.0, ((0, 8), (1, 4)), jnp.float32)
    moment2 = jnp.clip(jnp.exp(math.log(400.0) - 3.6888795 * jax.random.uniform(key_of[6], (N_DP, N_TENSOR * OWN, TILE * TILE), jnp.float32) ** block_levels(key_of[6], (N_DP, N_TENSOR * OWN, TILE * TILE), ((0, 8), (1, 4)), -0.2, 0.2)), 10.0, 400.0)
    return {"hidden_act": hidden_act, "out_grad": out_grad, "down_weight": down_weight, "kept_tiles": kept_tiles, "tile_owner": tile_owner, "moment1": moment1, "moment2": moment2}


beta_one = 0.9
beta_two = 0.95
eps_adam = 1e-08
learn_rate = 0.001

def tile_grads(operands):
    hid_rep, grad_rep, row_ids, col_ids = operands
    h_sel = jnp.take(hid_rep, row_ids.reshape(-1), axis=1).astype(jnp.float32)
    g_sel = jnp.take(grad_rep, col_ids.reshape(-1), axis=1).astype(jnp.float32)
    return jnp.einsum('npa,npb->pab', h_sel, g_sel).astype(jnp.bfloat16)

def reference(hidden_act, out_grad, down_weight, kept_tiles, tile_owner, moment1, moment2):
    grad_hidden = jnp.dot(out_grad, down_weight.T, preferred_element_type=jnp.float32).astype(jnp.bfloat16)
    kept = kept_tiles.reshape(N_DP, N_TENSOR, KEEP).astype(jnp.int32)
    shard_ids = jnp.arange(N_TENSOR, dtype=jnp.int32)[None, :, None]
    row_ids = (shard_ids * BLK_ROWS + kept // BLK_COLS).astype(jnp.int32)
    col_ids = (kept % BLK_COLS).astype(jnp.int32)
    hid_four = hidden_act.reshape(N_DP, TOK_DEV, HID // TILE, TILE)
    grad_four = out_grad.reshape(N_DP, TOK_DEV, BLK_COLS, TILE)
    pieces = lax.map(tile_grads, (hid_four, grad_four, row_ids, col_ids))
    flat_ids = (shard_ids * TILES_DEV + kept).reshape(-1).astype(jnp.int32)
    dense = jnp.zeros((N_TENSOR * TILES_DEV, TILE * TILE), jnp.float32)
    dense = dense.at[flat_ids].add(pieces.reshape(-1, TILE * TILE).astype(jnp.float32))
    owner = tile_owner.reshape(N_TENSOR, TILES_DEV)
    sorted_ids = jnp.argsort(owner, axis=1, stable=True).astype(jnp.int32)
    owned = sorted_ids.reshape(N_TENSOR, N_DP, OWN).transpose(1, 0, 2)
    take_ids = (shard_ids * TILES_DEV + owned).reshape(-1).astype(jnp.int32)
    merged = dense[take_ids].reshape(N_DP, N_TENSOR * OWN, TILE * TILE)
    moment1_new = beta_one * moment1 + (1.0 - beta_one) * merged
    moment2_new = beta_two * moment2 + (1.0 - beta_two) * merged * merged
    corr_one = 1.0 - beta_one ** STEP
    corr_two = 1.0 - beta_two ** STEP
    update = moment1_new / corr_one / (jnp.sqrt(moment2_new / corr_two) + eps_adam)
    weight_four = down_weight.reshape(HID // TILE, TILE, BLK_COLS, TILE)
    weight_rows = (shard_ids * BLK_ROWS + owned // BLK_COLS).astype(jnp.int32)
    weight_cols = (owned % BLK_COLS).astype(jnp.int32)
    current = weight_four[weight_rows, :, weight_cols, :]
    current = current.astype(jnp.float32).reshape(N_DP, N_TENSOR * OWN, TILE * TILE)
    weight_tiles = (current - learn_rate * update).astype(jnp.bfloat16)
    return (grad_hidden, moment1_new, moment2_new, weight_tiles)
```

```python
import functools

import jax
import jax.numpy as jnp
from jax import lax
from jax.experimental import pallas as pl
from jax.experimental.pallas import tpu as pltpu
from jax.sharding import PartitionSpec as P

TILE = 128
STEP = 10
CAP = 3
CHUNKS = 1
HID_BLK = 256
GROUP = 8

beta_one = 0.9
beta_two = 0.95
eps_adam = 1e-08
learn_rate = 0.001


def matmul_kernel(num, pos_ref, *refs):
    pieces = refs[: 2 * num]
    w_ref = refs[2 * num]
    out_ref, held = refs[-2], refs[-1]
    rows = pieces[0].shape[0]
    core = pos_ref[1]

    @pl.when(pl.program_id(0) == 0)
    def _():
        for k in range(num):
            mine = pl.multiple_of((core * num + k) * rows, rows)
            held[pl.ds(mine, rows), :] = pieces[k][...]
            other = pl.multiple_of(((1 - core) * num + k) * rows, rows)
            held[pl.ds(other, rows), :] = pieces[num + k][...]

    out_ref[...] = lax.dot_general(
        held[...], w_ref[...], (((1,), (1,)), ((), ())), preferred_element_type=jnp.float32
    ).astype(out_ref.dtype)


def grad_hidden_part(pos, pieces, weight, tok_rows, prev):
    num = len(pieces) // 2
    rows, width = pieces[0].shape
    hid = weight.shape[0]
    pair = 2 * num * rows
    in_specs = [pl.BlockSpec((rows, width), lambda j, s: (0, 0)) for _ in pieces]
    in_specs.append(pl.BlockSpec((HID_BLK, width), lambda j, s: (j, 0)))
    args = [pos, *pieces, weight]
    aliases = {}
    if prev is not None:
        in_specs.append(pl.BlockSpec(memory_space=pl.ANY))
        aliases = {len(args): 0}
        args.append(prev)
    return pl.pallas_call(
        functools.partial(matmul_kernel, num),
        out_shape=jax.ShapeDtypeStruct((tok_rows, hid), jnp.bfloat16),
        grid_spec=pltpu.PrefetchScalarGridSpec(
            num_scalar_prefetch=1,
            grid=(hid // HID_BLK,),
            in_specs=in_specs,
            out_specs=pl.BlockSpec((pair, HID_BLK), lambda j, s: (s[0], j)),
            scratch_shapes=[pltpu.VMEM((pair, width), jnp.bfloat16)],
        ),
        input_output_aliases=aliases,
        compiler_params=pltpu.CompilerParams(vmem_limit_bytes=40 * 2**20),
        cost_estimate=pl.CostEstimate(
            flops=2 * pair * width * hid, bytes_accessed=2 * hid * width, transcendentals=0
        ),
        name="grad_hidden",
    )(*args)


def tile_kernel(num, has_prev, last, pos_ref, *refs):
    h_ref = refs[0]
    pieces = refs[1 : 1 + 2 * num]
    rows = pieces[0].shape[0]
    core = pos_ref[1]
    total = None
    for k in range(2 * num):
        side = core if k < num else 1 - core
        start = pl.multiple_of((side * num + k % num) * rows, rows)
        term = lax.dot_general(
            h_ref[pl.ds(start, rows), :],
            pieces[k][...],
            (((0,), (0,)), ((), ())),
            preferred_element_type=jnp.float32,
        )
        total = term if total is None else total + term
    if has_prev:
        total = total + refs[1 + 2 * num][...]
    if not last:
        refs[-1][...] = total
        return
    outs = refs[1 + 2 * num + int(has_prev) : -1]
    pack = refs[-1]
    step = pl.program_id(0)
    kept_num = pl.num_programs(0)

    @pl.when(step == 0)
    def _():
        pack[...] = jnp.zeros_like(pack)

    place = pl.multiple_of(pos_ref[2 + 2 * kept_num + step] * TILE, TILE)
    pack[pl.ds(place, TILE), :] = total.astype(pack.dtype)

    @pl.when(step == kept_num - 1)
    def _():
        for d, out in enumerate(outs):
            out[...] = pack[d * CAP * TILE : (d + 1) * CAP * TILE, :]


def tile_part(pos, hidden_act, pieces, prev, kept_num, dp_size, last):
    num = len(pieces) // 2
    rows = pieces[0].shape[0]
    pair = 2 * num * rows
    in_specs = [pl.BlockSpec((pair, TILE), lambda p, s: (s[0], s[2 + p]))]
    in_specs += [
        pl.BlockSpec((rows, TILE), lambda p, s: (0, s[2 + kept_num + p])) for _ in pieces
    ]
    args = [pos, hidden_act, *pieces]
    if prev is not None:
        in_specs.append(pl.BlockSpec((None, TILE, TILE), lambda p, s: (p, 0, 0)))
        args.append(prev)
    scratch = []
    if last:
        out_shape = [jax.ShapeDtypeStruct((CAP * TILE, TILE), jnp.bfloat16)] * dp_size
        out_specs = [pl.BlockSpec((CAP * TILE, TILE), lambda p, s: (0, 0))] * dp_size
        scratch = [pltpu.VMEM((dp_size * CAP * TILE, TILE), jnp.bfloat16)]
    else:
        out_shape = jax.ShapeDtypeStruct((kept_num, TILE, TILE), jnp.float32)
        out_specs = pl.BlockSpec((None, TILE, TILE), lambda p, s: (p, 0, 0))
    return pl.pallas_call(
        functools.partial(tile_kernel, num, prev is not None, last),
        out_shape=out_shape,
        grid_spec=pltpu.PrefetchScalarGridSpec(
            num_scalar_prefetch=1,
            grid=(kept_num,),
            in_specs=in_specs,
            out_specs=out_specs,
            scratch_shapes=scratch,
        ),
        compiler_params=pltpu.CompilerParams(vmem_limit_bytes=16 * 2**20),
        cost_estimate=pl.CostEstimate(
            flops=2 * kept_num * pair * TILE * TILE,
            bytes_accessed=kept_num * pair * TILE * 4,
            transcendentals=0,
        ),
        name="tile_grads",
    )(*args)


def adam_kernel(dp_size, groups, rows_ref, cols_ref, slot_ref, *refs):
    got = refs[:dp_size]
    w_refs = refs[dp_size : dp_size + GROUP]
    m1_ref, m2_ref, m1_out, m2_out, w_out, acc, flat = refs[dp_size + GROUP :]
    step = pl.program_id(0)

    @pl.when(step == 0)
    def _():
        acc[...] = jnp.zeros_like(acc)
        for d in range(dp_size):
            for q in range(CAP):
                slot = slot_ref[d * CAP + q]

                @pl.when(slot >= 0)
                def _():
                    place = pl.ds(pl.multiple_of(slot * TILE, TILE), TILE)
                    acc[place, :] += got[d][q * TILE : (q + 1) * TILE, :].astype(jnp.float32)

    for j in range(GROUP):
        flat[j * TILE : (j + 1) * TILE, :] = w_refs[j][...].astype(jnp.float32)

    corr_one = 1.0 - beta_one**STEP
    corr_two = 1.0 - beta_two**STEP
    base = step * GROUP * TILE

    def body(a, carry):
        lanes = pl.ds(pl.multiple_of(a * TILE, TILE), TILE)
        merged = acc[pl.ds(base + a, GROUP, stride=TILE), :]
        current = flat[pl.ds(a, GROUP, stride=TILE), :]
        m1 = beta_one * m1_ref[0, :, lanes] + (1.0 - beta_one) * merged
        m2 = beta_two * m2_ref[0, :, lanes] + (1.0 - beta_two) * merged * merged
        update = m1 / (corr_one * (jnp.sqrt(m2 / corr_two) + eps_adam))
        m1_out[0, :, lanes] = m1
        m2_out[0, :, lanes] = m2
        w_out[0, :, lanes] = (current - learn_rate * update).astype(w_out.dtype)
        return carry

    lax.fori_loop(0, TILE, body, 0, unroll=8)


def adam(rows, cols, slots, got, weight, moment1, moment2):
    dp_size = len(got)
    _, own_count, flat_size = moment1.shape
    groups = rows.shape[0] // GROUP
    in_specs = [pl.BlockSpec((CAP * TILE, TILE), lambda i, r, c, s: (0, 0)) for _ in got]
    for j in range(GROUP):
        in_specs.append(
            pl.BlockSpec(
                (TILE, TILE), lambda i, r, c, s, j=j: (r[i * GROUP + j], c[i * GROUP + j])
            )
        )
    moment_spec = pl.BlockSpec((1, GROUP, flat_size), lambda i, r, c, s: (0, i, 0))
    in_specs += [moment_spec, moment_spec]
    return pl.pallas_call(
        functools.partial(adam_kernel, dp_size, groups),
        out_shape=[
            jax.ShapeDtypeStruct(moment1.shape, jnp.float32),
            jax.ShapeDtypeStruct(moment1.shape, jnp.float32),
            jax.ShapeDtypeStruct(moment1.shape, jnp.bfloat16),
        ],
        grid_spec=pltpu.PrefetchScalarGridSpec(
            num_scalar_prefetch=3,
            grid=(groups,),
            in_specs=in_specs,
            out_specs=[moment_spec, moment_spec, moment_spec],
            scratch_shapes=[
                pltpu.VMEM((groups * GROUP * TILE, TILE), jnp.float32),
                pltpu.VMEM((GROUP * TILE, TILE), jnp.float32),
            ],
        ),
        compiler_params=pltpu.CompilerParams(vmem_limit_bytes=24 * 2**20),
        cost_estimate=pl.CostEstimate(
            flops=20 * own_count * flat_size,
            bytes_accessed=20 * own_count * flat_size,
            transcendentals=own_count * flat_size,
        ),
        name="adam",
    )(rows, cols, slots, *got, *[weight] * GROUP, moment1, moment2)


def shards(hidden_act, out_grad, down_weight, kept_tiles, tile_owner, moment1, moment2):
    tok_rows = hidden_act.shape[0]
    blk_cols = down_weight.shape[1] // TILE
    own_count = moment1.shape[1]
    dp_size = lax.axis_size("dp")
    tensor_size = lax.axis_size("tensor")
    chips = tensor_size // 2
    me = lax.axis_index("dp").astype(jnp.int32)
    rank = lax.axis_index("tensor").astype(jnp.int32)
    chip, core = rank // 2, rank % 2

    swap = [(i, i ^ 1) for i in range(tensor_size)]
    part = out_grad.shape[0] // CHUNKS
    mine = [out_grad[k * part : (k + 1) * part] for k in range(CHUNKS)]
    far = []
    for hop in range(1, chips):
        ring = [(i, (i + 2 * hop) % tensor_size) for i in range(tensor_size)]
        far.append([lax.ppermute(piece, "tensor", ring) for piece in mine])
    near = [out_grad, lax.ppermute(out_grad, "tensor", swap)]
    groups = [near]
    for got in far:
        groups.append(got + [lax.ppermute(piece, "tensor", swap) for piece in got])

    kept = kept_tiles.reshape(-1)
    kept_num = kept.shape[0]
    owner = tile_owner.reshape(-1)
    numbers = jnp.arange(owner.shape[0], dtype=jnp.int32)
    before = (owner[:, None] == owner[None, :]) & (numbers[None, :] < numbers[:, None])
    slot_of = jnp.sum(before.astype(jnp.int32), axis=1)
    hit = kept[:, None] == numbers[None, :]
    kept_owner = jnp.sum(jnp.where(hit, owner[None, :], 0), axis=1)
    kept_slot = jnp.sum(jnp.where(hit, slot_of[None, :], 0), axis=1)
    order = jnp.arange(kept_num, dtype=jnp.int32)
    same = (kept_owner[:, None] == kept_owner[None, :]) & (order[None, :] < order[:, None])
    kept_rank = jnp.sum(same.astype(jnp.int32), axis=1)
    place = (kept_owner - me + dp_size) % dp_size * CAP + kept_rank
    seats = jnp.arange(dp_size * CAP, dtype=jnp.int32)
    sent_slots = (
        jnp.sum(jnp.where(place[None, :] == seats[:, None], kept_slot[None, :] + 1, 0), axis=1) - 1
    )
    padded = -(-own_count // GROUP) * GROUP
    mask = (owner == me)[None, :] & (
        slot_of[None, :] == jnp.arange(padded, dtype=jnp.int32)[:, None]
    )
    owned = jnp.sum(jnp.where(mask, numbers[None, :], 0), axis=1)

    slots = [sent_slots[:CAP]]
    for d in range(1, dp_size):
        ring = [(i, (i + d) % dp_size) for i in range(dp_size)]
        slots.append(lax.ppermute(sent_slots[d * CAP : (d + 1) * CAP], "dp", ring))
    slots = jnp.concatenate(slots)

    grad_hidden, partial = None, None
    for hop, pieces in enumerate(groups):
        source = (chip - hop + chips) % chips
        pos = jnp.concatenate(
            [jnp.stack([source, core]), kept // blk_cols, kept % blk_cols, place]
        )
        partial = tile_part(
            pos, hidden_act, pieces, partial, kept_num, dp_size, hop == chips - 1
        )
        grad_hidden = grad_hidden_part(pos, pieces, down_weight, tok_rows, grad_hidden)

    tiles = [partial[0]]
    for d in range(1, dp_size):
        ring = [(i, (i + d) % dp_size) for i in range(dp_size)]
        tiles.append(lax.ppermute(partial[d], "dp", ring))
    moment1_new, moment2_new, weight_tiles = adam(
        owned // blk_cols, owned % blk_cols, slots, tiles, down_weight, moment1, moment2
    )
    return (grad_hidden, moment1_new, moment2_new, weight_tiles)


def solution(mesh):
    in_specs = (
        P("dp", "tensor"),
        P(("dp", "tensor"), None),
        P("tensor", None),
        P("dp", "tensor"),
        P("tensor", None),
        P("dp", "tensor", None),
        P("dp", "tensor", None),
    )
    out_specs = (
        P("dp", "tensor"),
        P("dp", "tensor", None),
        P("dp", "tensor", None),
        P("dp", "tensor", None),
    )
    return jax.shard_map(shards, mesh=mesh, in_specs=in_specs, out_specs=out_specs, check_vma=False)
```

```python
import functools

import jax
import jax.numpy as jnp
from jax import lax
from jax.experimental import pallas as pl
from jax.experimental.pallas import tpu as pltpu
from jax.sharding import PartitionSpec as P

TILE = 128
STEP = 10
CAP = 3
CHUNKS = 2
PITCH = TILE + 8
HID_BLK = 256
GROUP = 8

beta_one = 0.9
beta_two = 0.95
eps_adam = 1e-08
learn_rate = 0.001


def matmul_kernel(num, pos_ref, *refs):
    pieces = refs[: 2 * num]
    w_ref = refs[2 * num]
    out_ref, held = refs[-2], refs[-1]
    rows = pieces[0].shape[0]
    core = pos_ref[1]

    @pl.when(pl.program_id(0) == 0)
    def _():
        for k in range(num):
            mine = pl.multiple_of((core * num + k) * rows, rows)
            held[pl.ds(mine, rows), :] = pieces[k][...]
            other = pl.multiple_of(((1 - core) * num + k) * rows, rows)
            held[pl.ds(other, rows), :] = pieces[num + k][...]

    out_ref[...] = lax.dot_general(
        held[...], w_ref[...], (((1,), (1,)), ((), ())), preferred_element_type=jnp.float32
    ).astype(out_ref.dtype)


def grad_hidden_part(pos, pieces, weight, tok_rows, prev):
    num = len(pieces) // 2
    rows, width = pieces[0].shape
    hid = weight.shape[0]
    pair = 2 * num * rows
    in_specs = [pl.BlockSpec((rows, width), lambda j, s: (0, 0)) for _ in pieces]
    in_specs.append(pl.BlockSpec((HID_BLK, width), lambda j, s: (j, 0)))
    args = [pos, *pieces, weight]
    aliases = {}
    if prev is not None:
        in_specs.append(pl.BlockSpec(memory_space=pl.ANY))
        aliases = {len(args): 0}
        args.append(prev)
    return pl.pallas_call(
        functools.partial(matmul_kernel, num),
        out_shape=jax.ShapeDtypeStruct((tok_rows, hid), jnp.bfloat16),
        grid_spec=pltpu.PrefetchScalarGridSpec(
            num_scalar_prefetch=1,
            grid=(hid // HID_BLK,),
            in_specs=in_specs,
            out_specs=pl.BlockSpec((pair, HID_BLK), lambda j, s: (s[0], j)),
            scratch_shapes=[pltpu.VMEM((pair, width), jnp.bfloat16)],
        ),
        input_output_aliases=aliases,
        compiler_params=pltpu.CompilerParams(vmem_limit_bytes=40 * 2**20),
        cost_estimate=pl.CostEstimate(
            flops=2 * pair * width * hid, bytes_accessed=2 * hid * width, transcendentals=0
        ),
        name="grad_hidden",
    )(*args)


def tile_kernel(has_prev, last, pos_ref, *refs):
    h_mine, h_other, g_mine, g_other = refs[:4]
    dims = (((0,), (0,)), ((), ()))
    total = lax.dot_general(h_mine[...], g_mine[...], dims, preferred_element_type=jnp.float32)
    total += lax.dot_general(h_other[...], g_other[...], dims, preferred_element_type=jnp.float32)
    if has_prev:
        total = total + refs[4][...]
    if not last:
        refs[-1][...] = total
        return
    outs = refs[4 + int(has_prev) : -1]
    pack = refs[-1]
    step = pl.program_id(0)
    kept_num = pl.num_programs(0)

    @pl.when(step == 0)
    def _():
        pack[...] = jnp.zeros_like(pack)

    place = pl.multiple_of(pos_ref[2 + 2 * kept_num + step] * TILE, TILE)
    pack[pl.ds(place, TILE), :] = total.astype(pack.dtype)

    @pl.when(step == kept_num - 1)
    def _():
        for d, out in enumerate(outs):
            out[...] = pack[d * CAP * TILE : (d + 1) * CAP * TILE, :]


def tile_part(pos, hidden_act, pieces, prev, kept_num, dp_size, last):
    rows = pieces[0].shape[0]
    in_specs = [
        pl.BlockSpec((rows, TILE), lambda p, s: (s[0], s[2 + p])),
        pl.BlockSpec((rows, TILE), lambda p, s: (s[1], s[2 + p])),
        pl.BlockSpec((rows, TILE), lambda p, s: (0, s[2 + kept_num + p])),
        pl.BlockSpec((rows, TILE), lambda p, s: (0, s[2 + kept_num + p])),
    ]
    args = [pos, hidden_act, hidden_act, *pieces]
    if prev is not None:
        in_specs.append(pl.BlockSpec((None, TILE, TILE), lambda p, s: (p, 0, 0)))
        args.append(prev)
    scratch = []
    if last:
        out_shape = [jax.ShapeDtypeStruct((CAP * TILE, TILE), jnp.bfloat16)] * dp_size
        out_specs = [pl.BlockSpec((CAP * TILE, TILE), lambda p, s: (0, 0))] * dp_size
        scratch = [pltpu.VMEM((dp_size * CAP * TILE, TILE), jnp.bfloat16)]
    else:
        out_shape = jax.ShapeDtypeStruct((kept_num, TILE, TILE), jnp.float32)
        out_specs = pl.BlockSpec((None, TILE, TILE), lambda p, s: (p, 0, 0))
    return pl.pallas_call(
        functools.partial(tile_kernel, prev is not None, last),
        out_shape=out_shape,
        grid_spec=pltpu.PrefetchScalarGridSpec(
            num_scalar_prefetch=1,
            grid=(kept_num,),
            in_specs=in_specs,
            out_specs=out_specs,
            scratch_shapes=scratch,
        ),
        compiler_params=pltpu.CompilerParams(vmem_limit_bytes=16 * 2**20),
        cost_estimate=pl.CostEstimate(
            flops=4 * kept_num * rows * TILE * TILE,
            bytes_accessed=8 * kept_num * rows * TILE,
            transcendentals=0,
        ),
        name="tile_grads",
    )(*args)


def adam_kernel(dp_size, groups, rows_ref, cols_ref, slot_ref, *refs):
    got = refs[:dp_size]
    w_refs = refs[dp_size : dp_size + GROUP]
    m1_ref, m2_ref, m1_out, m2_out, w_out, acc, flat = refs[dp_size + GROUP :]
    step = pl.program_id(0)

    @pl.when(step == 0)
    def _():
        acc[...] = jnp.zeros_like(acc)
        for d in range(dp_size):
            for q in range(CAP):
                slot = slot_ref[d * CAP + q]

                @pl.when(slot >= 0)
                def _():
                    place = pl.ds(pl.multiple_of(slot * PITCH, 8), TILE)
                    acc[place, :] += got[d][q * TILE : (q + 1) * TILE, :].astype(jnp.float32)

    for j in range(GROUP):
        flat[j * PITCH : j * PITCH + TILE, :] = w_refs[j][...].astype(jnp.float32)

    corr_one = 1.0 - beta_one**STEP
    corr_two = 1.0 - beta_two**STEP
    base = step * GROUP * PITCH

    def body(a, carry):
        lanes = pl.ds(pl.multiple_of(a * TILE, TILE), TILE)
        merged = acc[pl.ds(base + a, GROUP, stride=PITCH), :]
        current = flat[pl.ds(a, GROUP, stride=PITCH), :]
        m1 = beta_one * m1_ref[0, :, lanes] + (1.0 - beta_one) * merged
        m2 = beta_two * m2_ref[0, :, lanes] + (1.0 - beta_two) * merged * merged
        update = m1 / (corr_one * (jnp.sqrt(m2 / corr_two) + eps_adam))
        m1_out[0, :, lanes] = m1
        m2_out[0, :, lanes] = m2
        w_out[0, :, lanes] = (current - learn_rate * update).astype(w_out.dtype)
        return carry

    lax.fori_loop(0, TILE, body, 0, unroll=8)


def adam(rows, cols, slots, got, weight, moment1, moment2):
    dp_size = len(got)
    _, own_count, flat_size = moment1.shape
    groups = rows.shape[0] // GROUP
    in_specs = [pl.BlockSpec((CAP * TILE, TILE), lambda i, r, c, s: (0, 0)) for _ in got]
    for j in range(GROUP):
        in_specs.append(
            pl.BlockSpec(
                (TILE, TILE), lambda i, r, c, s, j=j: (r[i * GROUP + j], c[i * GROUP + j])
            )
        )
    moment_spec = pl.BlockSpec((1, GROUP, flat_size), lambda i, r, c, s: (0, i, 0))
    in_specs += [moment_spec, moment_spec]
    return pl.pallas_call(
        functools.partial(adam_kernel, dp_size, groups),
        out_shape=[
            jax.ShapeDtypeStruct(moment1.shape, jnp.float32),
            jax.ShapeDtypeStruct(moment1.shape, jnp.float32),
            jax.ShapeDtypeStruct(moment1.shape, jnp.bfloat16),
        ],
        grid_spec=pltpu.PrefetchScalarGridSpec(
            num_scalar_prefetch=3,
            grid=(groups,),
            in_specs=in_specs,
            out_specs=[moment_spec, moment_spec, moment_spec],
            scratch_shapes=[
                pltpu.VMEM((groups * GROUP * PITCH, TILE), jnp.float32),
                pltpu.VMEM((GROUP * PITCH, TILE), jnp.float32),
            ],
        ),
        compiler_params=pltpu.CompilerParams(vmem_limit_bytes=24 * 2**20),
        cost_estimate=pl.CostEstimate(
            flops=20 * own_count * flat_size,
            bytes_accessed=20 * own_count * flat_size,
            transcendentals=own_count * flat_size,
        ),
        name="adam",
    )(rows, cols, slots, *got, *[weight] * GROUP, moment1, moment2)


def shards(hidden_act, out_grad, down_weight, kept_tiles, tile_owner, moment1, moment2):
    tok_rows = hidden_act.shape[0]
    blk_cols = down_weight.shape[1] // TILE
    own_count = moment1.shape[1]
    dp_size = lax.axis_size("dp")
    tensor_size = lax.axis_size("tensor")
    chips = tensor_size // 2
    me = lax.axis_index("dp").astype(jnp.int32)
    rank = lax.axis_index("tensor").astype(jnp.int32)
    chip, core = rank // 2, rank % 2

    kept = kept_tiles.reshape(-1)
    kept_num = kept.shape[0]
    everyone = kept
    reach = 1
    while reach < dp_size:
        ring = [(i, (i + reach) % dp_size) for i in range(dp_size)]
        more = everyone[: (min(2 * reach, dp_size) - reach) * kept_num]
        everyone = jnp.concatenate([everyone, lax.ppermute(more, "dp", ring)])
        reach *= 2

    swap = [(i, i ^ 1) for i in range(tensor_size)]
    shard = out_grad.shape[0]
    part = shard // CHUNKS
    mine = [out_grad[k * part : (k + 1) * part] for k in range(CHUNKS)]
    far = []
    for hop in range(1, chips):
        ring = [(i, (i + 2 * hop) % tensor_size) for i in range(tensor_size)]
        far.append([lax.ppermute(piece, "tensor", ring) for piece in mine])

    owner = tile_owner.reshape(-1)
    numbers = jnp.arange(owner.shape[0], dtype=jnp.int32)
    before = (owner[:, None] == owner[None, :]) & (numbers[None, :] < numbers[:, None])
    slot_of = jnp.sum(before.astype(jnp.int32), axis=1)
    hit = everyone[:, None] == numbers[None, :]
    kept_owner = jnp.sum(jnp.where(hit, owner[None, :], 0), axis=1).reshape(dp_size, kept_num)
    kept_slot = jnp.sum(jnp.where(hit, slot_of[None, :], 0), axis=1).reshape(dp_size, kept_num)
    order = jnp.arange(kept_num, dtype=jnp.int32)
    same = (kept_owner[:, :, None] == kept_owner[:, None, :]) & (
        order[None, None, :] < order[None, :, None]
    )
    kept_rank = jnp.sum(same.astype(jnp.int32), axis=2)
    place = (kept_owner[0] - me + dp_size) % dp_size * CAP + kept_rank[0]
    seats = jnp.arange(CAP, dtype=jnp.int32)[None, :, None]
    seated = (kept_owner == me)[:, None, :] & (kept_rank[:, None, :] == seats)
    slots = jnp.sum(jnp.where(seated, kept_slot[:, None, :] + 1, 0), axis=2).reshape(-1) - 1
    padded = -(-own_count // GROUP) * GROUP
    mask = (owner == me)[None, :] & (
        slot_of[None, :] == jnp.arange(padded, dtype=jnp.int32)[:, None]
    )
    owned = jnp.sum(jnp.where(mask, numbers[None, :], 0), axis=1)

    def block_pos(source, chunk, count):
        side = source * 2
        blocks = [(side + core) * count + chunk, (side + 1 - core) * count + chunk]
        return jnp.concatenate([jnp.stack(blocks), kept // blk_cols, kept % blk_cols, place])

    near = [out_grad, lax.ppermute(out_grad, "tensor", swap)]
    partial = tile_part(
        block_pos(chip, 0, 1), hidden_act, near, None, kept_num, dp_size, chips == 1
    )
    grad_hidden = grad_hidden_part(
        jnp.stack([chip, core]), near, down_weight, tok_rows, None
    )
    for hop, got in enumerate(far, 1):
        source = (chip - hop + chips) % chips
        pieces = []
        for k, piece in enumerate(got):
            if k == CHUNKS - 1:
                piece, partial, grad_hidden, owned, slots = lax.optimization_barrier(
                    (piece, partial, grad_hidden, owned, slots)
                )
            else:
                piece, partial = lax.optimization_barrier((piece, partial))
            pieces.append([piece, lax.ppermute(piece, "tensor", swap)])
            partial = tile_part(
                block_pos(source, k, CHUNKS),
                hidden_act,
                pieces[k],
                partial,
                kept_num,
                dp_size,
                hop == chips - 1 and k == CHUNKS - 1,
            )
        ordered = [pair[0] for pair in pieces] + [pair[1] for pair in pieces]
        grad_hidden = grad_hidden_part(
            jnp.stack([source, core]), ordered, down_weight, tok_rows, grad_hidden
        )

    tiles = [partial[0]]
    for d in range(1, dp_size):
        ring = [(i, (i + d) % dp_size) for i in range(dp_size)]
        tiles.append(lax.ppermute(partial[d], "dp", ring))
    moment1_new, moment2_new, weight_tiles = adam(
        owned // blk_cols, owned % blk_cols, slots, tiles, down_weight, moment1, moment2
    )
    return (grad_hidden, moment1_new, moment2_new, weight_tiles)


def solution(mesh):
    in_specs = (
        P("dp", "tensor"),
        P(("dp", "tensor"), None),
        P("tensor", None),
        P("dp", "tensor"),
        P("tensor", None),
        P("dp", "tensor", None),
        P("dp", "tensor", None),
    )
    out_specs = (
        P("dp", "tensor"),
        P("dp", "tensor", None),
        P("dp", "tensor", None),
        P("dp", "tensor", None),
    )
    return jax.shard_map(shards, mesh=mesh, in_specs=in_specs, out_specs=out_specs, check_vma=False)
```

```python
import functools

import jax
import jax.numpy as jnp
from jax import lax
from jax.experimental import pallas as pl
from jax.experimental.pallas import tpu as pltpu
from jax.sharding import PartitionSpec as P

TILE = 128
STEP = 10
CAP = 3
CHUNKS = 1
PITCH = TILE + 8
HID_BLK = 256
GROUP = 8

beta_one = 0.9
beta_two = 0.95
eps_adam = 1e-08
learn_rate = 0.001


def matmul_kernel(num, pos_ref, *refs):
    pieces = refs[: 2 * num]
    w_ref = refs[2 * num]
    out_ref, held = refs[-2], refs[-1]
    rows = pieces[0].shape[0]
    core = pos_ref[1]

    @pl.when(pl.program_id(0) == 0)
    def _():
        for k in range(num):
            mine = pl.multiple_of((core * num + k) * rows, rows)
            held[pl.ds(mine, rows), :] = pieces[k][...]
            other = pl.multiple_of(((1 - core) * num + k) * rows, rows)
            held[pl.ds(other, rows), :] = pieces[num + k][...]

    out_ref[...] = lax.dot_general(
        held[...], w_ref[...], (((1,), (1,)), ((), ())), preferred_element_type=jnp.float32
    ).astype(out_ref.dtype)


def grad_hidden_part(pos, pieces, weight, tok_rows, prev):
    num = len(pieces) // 2
    rows, width = pieces[0].shape
    hid = weight.shape[0]
    pair = 2 * num * rows
    in_specs = [pl.BlockSpec((rows, width), lambda j, s: (0, 0)) for _ in pieces]
    in_specs.append(pl.BlockSpec((HID_BLK, width), lambda j, s: (j, 0)))
    args = [pos, *pieces, weight]
    aliases = {}
    if prev is not None:
        in_specs.append(pl.BlockSpec(memory_space=pl.ANY))
        aliases = {len(args): 0}
        args.append(prev)
    return pl.pallas_call(
        functools.partial(matmul_kernel, num),
        out_shape=jax.ShapeDtypeStruct((tok_rows, hid), jnp.bfloat16),
        grid_spec=pltpu.PrefetchScalarGridSpec(
            num_scalar_prefetch=1,
            grid=(hid // HID_BLK,),
            in_specs=in_specs,
            out_specs=pl.BlockSpec((pair, HID_BLK), lambda j, s: (s[0], j)),
            scratch_shapes=[pltpu.VMEM((pair, width), jnp.bfloat16)],
        ),
        input_output_aliases=aliases,
        compiler_params=pltpu.CompilerParams(vmem_limit_bytes=40 * 2**20),
        cost_estimate=pl.CostEstimate(
            flops=2 * pair * width * hid, bytes_accessed=2 * hid * width, transcendentals=0
        ),
        name="grad_hidden",
    )(*args)


def turn_kernel(pos_ref, h_ref, out_ref):
    out_ref[...] = h_ref[...].T


def turned_tiles(kept_rows, hidden_act):
    kept_num = kept_rows.shape[0]
    tokens = hidden_act.shape[0]
    return pl.pallas_call(
        turn_kernel,
        out_shape=jax.ShapeDtypeStruct((kept_num * TILE, tokens), jnp.bfloat16),
        grid_spec=pltpu.PrefetchScalarGridSpec(
            num_scalar_prefetch=1,
            grid=(kept_num,),
            in_specs=[pl.BlockSpec((tokens, TILE), lambda p, s: (0, s[p]))],
            out_specs=pl.BlockSpec((TILE, tokens), lambda p, s: (p, 0)),
        ),
        compiler_params=pltpu.CompilerParams(vmem_limit_bytes=8 * 2**20),
        cost_estimate=pl.CostEstimate(
            flops=0, bytes_accessed=16 * kept_num * tokens * TILE, transcendentals=0
        ),
        name="turned_tiles",
    )(kept_rows, hidden_act)


def tile_kernel(kept_num, has_prev, last, pos_ref, h_ref, g_mine, g_other, *refs):
    rows = g_mine.shape[0]
    mine = pl.ds(pl.multiple_of(pos_ref[0] * rows, rows), rows)
    other = pl.ds(pl.multiple_of(pos_ref[1] * rows, rows), rows)
    outs = refs[int(has_prev) : -1]
    pack = refs[-1]
    if last:
        pack[...] = jnp.zeros_like(pack)
    for p in range(kept_num):
        tile = pl.ds(p * TILE, TILE)
        lanes = pl.ds(pl.multiple_of(pos_ref[2 + p] * TILE, TILE), TILE)
        total = jnp.dot(h_ref[tile, mine], g_mine[:, lanes], preferred_element_type=jnp.float32)
        total += jnp.dot(h_ref[tile, other], g_other[:, lanes], preferred_element_type=jnp.float32)
        if has_prev:
            total = total + refs[0][tile, :]
        if last:
            place = pl.multiple_of(pos_ref[2 + kept_num + p] * TILE, TILE)
            pack[pl.ds(place, TILE), :] = total.astype(pack.dtype)
        else:
            refs[-1][tile, :] = total
    if last:
        for d, out in enumerate(outs):
            out[...] = pack[d * CAP * TILE : (d + 1) * CAP * TILE, :]


def tile_part(pos, turned, pieces, prev, kept_num, dp_size, last):
    rows = pieces[0].shape[0]
    args = [pos, turned, *pieces]
    if prev is not None:
        args.append(prev)
    scratch = []
    if last:
        out_shape = [jax.ShapeDtypeStruct((CAP * TILE, TILE), jnp.bfloat16)] * dp_size
        scratch = [pltpu.VMEM((dp_size * CAP * TILE, TILE), jnp.bfloat16)]
    else:
        out_shape = jax.ShapeDtypeStruct((kept_num * TILE, TILE), jnp.float32)
    whole = pl.BlockSpec(memory_space=pltpu.VMEM)
    return pl.pallas_call(
        functools.partial(tile_kernel, kept_num, prev is not None, last),
        out_shape=out_shape,
        in_specs=[pl.BlockSpec(memory_space=pltpu.SMEM)] + [whole] * (len(args) - 1),
        out_specs=[whole] * dp_size if last else whole,
        scratch_shapes=scratch,
        compiler_params=pltpu.CompilerParams(vmem_limit_bytes=24 * 2**20),
        cost_estimate=pl.CostEstimate(
            flops=4 * kept_num * rows * TILE * TILE,
            bytes_accessed=8 * kept_num * rows * TILE,
            transcendentals=0,
        ),
        name="tile_grads",
    )(*args)


def adam_kernel(dp_size, groups, rows_ref, cols_ref, slot_ref, *refs):
    got = refs[:dp_size]
    w_refs = refs[dp_size : dp_size + GROUP]
    m1_ref, m2_ref, m1_out, m2_out, w_out, acc, flat = refs[dp_size + GROUP :]
    step = pl.program_id(0)

    @pl.when(step == 0)
    def _():
        acc[...] = jnp.zeros_like(acc)
        for d in range(dp_size):
            for q in range(CAP):
                slot = slot_ref[d * CAP + q]

                @pl.when(slot >= 0)
                def _():
                    place = pl.ds(pl.multiple_of(slot * PITCH, 8), TILE)
                    acc[place, :] += got[d][q * TILE : (q + 1) * TILE, :].astype(jnp.float32)

    for j in range(GROUP):
        flat[j * PITCH : j * PITCH + TILE, :] = w_refs[j][...].astype(jnp.float32)

    corr_one = 1.0 - beta_one**STEP
    corr_two = 1.0 - beta_two**STEP
    base = step * GROUP * PITCH

    def body(a, carry):
        lanes = pl.ds(pl.multiple_of(a * TILE, TILE), TILE)
        merged = acc[pl.ds(base + a, GROUP, stride=PITCH), :]
        current = flat[pl.ds(a, GROUP, stride=PITCH), :]
        m1 = beta_one * m1_ref[0, :, lanes] + (1.0 - beta_one) * merged
        m2 = beta_two * m2_ref[0, :, lanes] + (1.0 - beta_two) * merged * merged
        update = m1 / (corr_one * (jnp.sqrt(m2 / corr_two) + eps_adam))
        m1_out[0, :, lanes] = m1
        m2_out[0, :, lanes] = m2
        w_out[0, :, lanes] = (current - learn_rate * update).astype(w_out.dtype)
        return carry

    lax.fori_loop(0, TILE, body, 0, unroll=8)


def adam(rows, cols, slots, got, weight, moment1, moment2):
    dp_size = len(got)
    _, own_count, flat_size = moment1.shape
    groups = rows.shape[0] // GROUP
    in_specs = [pl.BlockSpec((CAP * TILE, TILE), lambda i, r, c, s: (0, 0)) for _ in got]
    for j in range(GROUP):
        in_specs.append(
            pl.BlockSpec(
                (TILE, TILE), lambda i, r, c, s, j=j: (r[i * GROUP + j], c[i * GROUP + j])
            )
        )
    moment_spec = pl.BlockSpec((1, GROUP, flat_size), lambda i, r, c, s: (0, i, 0))
    in_specs += [moment_spec, moment_spec]
    return pl.pallas_call(
        functools.partial(adam_kernel, dp_size, groups),
        out_shape=[
            jax.ShapeDtypeStruct(moment1.shape, jnp.float32),
            jax.ShapeDtypeStruct(moment1.shape, jnp.float32),
            jax.ShapeDtypeStruct(moment1.shape, jnp.bfloat16),
        ],
        grid_spec=pltpu.PrefetchScalarGridSpec(
            num_scalar_prefetch=3,
            grid=(groups,),
            in_specs=in_specs,
            out_specs=[moment_spec, moment_spec, moment_spec],
            scratch_shapes=[
                pltpu.VMEM((groups * GROUP * PITCH, TILE), jnp.float32),
                pltpu.VMEM((GROUP * PITCH, TILE), jnp.float32),
            ],
        ),
        compiler_params=pltpu.CompilerParams(vmem_limit_bytes=24 * 2**20),
        cost_estimate=pl.CostEstimate(
            flops=20 * own_count * flat_size,
            bytes_accessed=20 * own_count * flat_size,
            transcendentals=own_count * flat_size,
        ),
        name="adam",
    )(rows, cols, slots, *got, *[weight] * GROUP, moment1, moment2)


def shards(hidden_act, out_grad, down_weight, kept_tiles, tile_owner, moment1, moment2):
    tok_rows = hidden_act.shape[0]
    blk_cols = down_weight.shape[1] // TILE
    own_count = moment1.shape[1]
    dp_size = lax.axis_size("dp")
    tensor_size = lax.axis_size("tensor")
    chips = tensor_size // 2
    me = lax.axis_index("dp").astype(jnp.int32)
    rank = lax.axis_index("tensor").astype(jnp.int32)
    chip, core = rank // 2, rank % 2

    kept = kept_tiles.reshape(-1)
    kept_num = kept.shape[0]
    everyone = kept
    reach = 1
    while reach < dp_size:
        ring = [(i, (i + reach) % dp_size) for i in range(dp_size)]
        more = everyone[: (min(2 * reach, dp_size) - reach) * kept_num]
        everyone = jnp.concatenate([everyone, lax.ppermute(more, "dp", ring)])
        reach *= 2

    swap = [(i, i ^ 1) for i in range(tensor_size)]
    shard = out_grad.shape[0]
    part = shard // CHUNKS
    mine = [out_grad[k * part : (k + 1) * part] for k in range(CHUNKS)]
    far = []
    for hop in range(1, chips):
        ring = [(i, (i + 2 * hop) % tensor_size) for i in range(tensor_size)]
        far.append([lax.ppermute(piece, "tensor", ring) for piece in mine])

    owner = tile_owner.reshape(-1)
    numbers = jnp.arange(owner.shape[0], dtype=jnp.int32)
    before = (owner[:, None] == owner[None, :]) & (numbers[None, :] < numbers[:, None])
    slot_of = jnp.sum(before.astype(jnp.int32), axis=1)
    hit = everyone[:, None] == numbers[None, :]
    kept_owner = jnp.sum(jnp.where(hit, owner[None, :], 0), axis=1).reshape(dp_size, kept_num)
    kept_slot = jnp.sum(jnp.where(hit, slot_of[None, :], 0), axis=1).reshape(dp_size, kept_num)
    order = jnp.arange(kept_num, dtype=jnp.int32)
    same = (kept_owner[:, :, None] == kept_owner[:, None, :]) & (
        order[None, None, :] < order[None, :, None]
    )
    kept_rank = jnp.sum(same.astype(jnp.int32), axis=2)
    place = (kept_owner[0] - me + dp_size) % dp_size * CAP + kept_rank[0]
    seats = jnp.arange(CAP, dtype=jnp.int32)[None, :, None]
    seated = (kept_owner == me)[:, None, :] & (kept_rank[:, None, :] == seats)
    slots = jnp.sum(jnp.where(seated, kept_slot[:, None, :] + 1, 0), axis=2).reshape(-1) - 1
    padded = -(-own_count // GROUP) * GROUP
    mask = (owner == me)[None, :] & (
        slot_of[None, :] == jnp.arange(padded, dtype=jnp.int32)[:, None]
    )
    owned = jnp.sum(jnp.where(mask, numbers[None, :], 0), axis=1)

    def block_pos(source, chunk, count):
        side = source * 2
        blocks = [(side + core) * count + chunk, (side + 1 - core) * count + chunk]
        return jnp.concatenate([jnp.stack(blocks), kept % blk_cols, place])

    turned = turned_tiles(kept // blk_cols, hidden_act)
    near = [out_grad, lax.ppermute(out_grad, "tensor", swap)]
    partial = tile_part(
        block_pos(chip, 0, 1), turned, near, None, kept_num, dp_size, chips == 1
    )
    grad_hidden = grad_hidden_part(
        jnp.stack([chip, core]), near, down_weight, tok_rows, None
    )
    for hop, got in enumerate(far, 1):
        source = (chip - hop + chips) % chips
        pieces = []
        for k, piece in enumerate(got):
            if k == CHUNKS - 1:
                piece, partial, grad_hidden, owned, slots = lax.optimization_barrier(
                    (piece, partial, grad_hidden, owned, slots)
                )
            else:
                piece, partial = lax.optimization_barrier((piece, partial))
            pieces.append([piece, lax.ppermute(piece, "tensor", swap)])
            partial = tile_part(
                block_pos(source, k, CHUNKS),
                turned,
                pieces[k],
                partial,
                kept_num,
                dp_size,
                hop == chips - 1 and k == CHUNKS - 1,
            )
        ordered = [pair[0] for pair in pieces] + [pair[1] for pair in pieces]
        grad_hidden = grad_hidden_part(
            jnp.stack([source, core]), ordered, down_weight, tok_rows, grad_hidden
        )

    tiles = [partial[0]]
    for d in range(1, dp_size):
        ring = [(i, (i + d) % dp_size) for i in range(dp_size)]
        tiles.append(lax.ppermute(partial[d], "dp", ring))
    moment1_new, moment2_new, weight_tiles = adam(
        owned // blk_cols, owned % blk_cols, slots, tiles, down_weight, moment1, moment2
    )
    return (grad_hidden, moment1_new, moment2_new, weight_tiles)


def solution(mesh):
    in_specs = (
        P("dp", "tensor"),
        P(("dp", "tensor"), None),
        P("tensor", None),
        P("dp", "tensor"),
        P("tensor", None),
        P("dp", "tensor", None),
        P("dp", "tensor", None),
    )
    out_specs = (
        P("dp", "tensor"),
        P("dp", "tensor", None),
        P("dp", "tensor", None),
        P("dp", "tensor", None),
    )
    return jax.shard_map(shards, mesh=mesh, in_specs=in_specs, out_specs=out_specs, check_vma=False)
```

```python
import functools

import jax
import jax.numpy as jnp
from jax import lax
from jax.experimental import pallas as pl
from jax.experimental.pallas import tpu as pltpu
from jax.sharding import PartitionSpec as P

TILE = 128
STEP = 10
CAP = 3
CHUNKS = 1
PITCH = TILE + 8
HID_BLK = 256
GROUP = 8

beta_one = 0.9
beta_two = 0.95
eps_adam = 1e-08
learn_rate = 0.001


def matmul_kernel(num, pos_ref, *refs):
    pieces = refs[: 2 * num]
    w_ref = refs[2 * num]
    out_ref, held = refs[-2], refs[-1]
    rows = pieces[0].shape[0]
    core = pos_ref[1]

    @pl.when(pl.program_id(0) == 0)
    def _():
        for k in range(num):
            mine = pl.multiple_of((core * num + k) * rows, rows)
            held[pl.ds(mine, rows), :] = pieces[k][...]
            other = pl.multiple_of(((1 - core) * num + k) * rows, rows)
            held[pl.ds(other, rows), :] = pieces[num + k][...]

    out_ref[...] = lax.dot_general(
        held[...], w_ref[...], (((1,), (1,)), ((), ())), preferred_element_type=jnp.float32
    ).astype(out_ref.dtype)


def grad_hidden_part(pos, pieces, weight, tok_rows, prev):
    num = len(pieces) // 2
    rows, width = pieces[0].shape
    hid = weight.shape[0]
    pair = 2 * num * rows
    in_specs = [pl.BlockSpec((rows, width), lambda j, s: (0, 0)) for _ in pieces]
    in_specs.append(pl.BlockSpec((HID_BLK, width), lambda j, s: (j, 0)))
    args = [pos, *pieces, weight]
    aliases = {}
    if prev is not None:
        in_specs.append(pl.BlockSpec(memory_space=pl.ANY))
        aliases = {len(args): 0}
        args.append(prev)
    return pl.pallas_call(
        functools.partial(matmul_kernel, num),
        out_shape=jax.ShapeDtypeStruct((tok_rows, hid), jnp.bfloat16),
        grid_spec=pltpu.PrefetchScalarGridSpec(
            num_scalar_prefetch=1,
            grid=(hid // HID_BLK,),
            in_specs=in_specs,
            out_specs=pl.BlockSpec((pair, HID_BLK), lambda j, s: (s[0], j)),
            scratch_shapes=[pltpu.VMEM((pair, width), jnp.bfloat16)],
        ),
        input_output_aliases=aliases,
        compiler_params=pltpu.CompilerParams(vmem_limit_bytes=40 * 2**20),
        cost_estimate=pl.CostEstimate(
            flops=2 * pair * width * hid, bytes_accessed=2 * hid * width, transcendentals=0
        ),
        name="grad_hidden",
    )(*args)


def turn_kernel(pos_ref, h_ref, out_ref):
    out_ref[...] = h_ref[...].T


def turned_tiles(kept_rows, hidden_act):
    kept_num = kept_rows.shape[0]
    tokens = hidden_act.shape[0]
    return pl.pallas_call(
        turn_kernel,
        out_shape=jax.ShapeDtypeStruct((kept_num * TILE, tokens), jnp.bfloat16),
        grid_spec=pltpu.PrefetchScalarGridSpec(
            num_scalar_prefetch=1,
            grid=(kept_num,),
            in_specs=[pl.BlockSpec((tokens, TILE), lambda p, s: (0, s[p]))],
            out_specs=pl.BlockSpec((TILE, tokens), lambda p, s: (p, 0)),
        ),
        compiler_params=pltpu.CompilerParams(vmem_limit_bytes=8 * 2**20),
        cost_estimate=pl.CostEstimate(
            flops=0, bytes_accessed=16 * kept_num * tokens * TILE, transcendentals=0
        ),
        name="turned_tiles",
    )(kept_rows, hidden_act)


def tile_kernel(kept_num, has_prev, last, pos_ref, h_ref, g_mine, g_other, *refs):
    rows = g_mine.shape[0]
    mine = pl.ds(pl.multiple_of(pos_ref[0] * rows, rows), rows)
    other = pl.ds(pl.multiple_of(pos_ref[1] * rows, rows), rows)
    pack = refs[-1]
    if last:
        pack[...] = jnp.zeros_like(pack)
    for p in range(kept_num):
        tile = pl.ds(p * TILE, TILE)
        lanes = pl.ds(pl.multiple_of(pos_ref[2 + p] * TILE, TILE), TILE)
        total = jnp.dot(h_ref[tile, mine], g_mine[:, lanes], preferred_element_type=jnp.float32)
        total += jnp.dot(h_ref[tile, other], g_other[:, lanes], preferred_element_type=jnp.float32)
        if has_prev:
            total = total + refs[0][tile, :]
        if last:
            place = pl.multiple_of(pos_ref[2 + kept_num + p] * TILE, TILE)
            pack[pl.ds(place, TILE), :] = total.astype(pack.dtype)
        else:
            refs[-1][tile, :] = total


def tile_part(pos, turned, pieces, prev, kept_num, dp_size, last):
    rows = pieces[0].shape[0]
    args = [pos, turned, *pieces]
    if prev is not None:
        args.append(prev)
    if last:
        out_shape = jax.ShapeDtypeStruct((dp_size * CAP * TILE, TILE), jnp.bfloat16)
    else:
        out_shape = jax.ShapeDtypeStruct((kept_num * TILE, TILE), jnp.float32)
    whole = pl.BlockSpec(memory_space=pltpu.VMEM)
    return pl.pallas_call(
        functools.partial(tile_kernel, kept_num, prev is not None, last),
        out_shape=out_shape,
        in_specs=[pl.BlockSpec(memory_space=pltpu.SMEM)] + [whole] * (len(args) - 1),
        out_specs=whole,
        compiler_params=pltpu.CompilerParams(vmem_limit_bytes=24 * 2**20),
        cost_estimate=pl.CostEstimate(
            flops=4 * kept_num * rows * TILE * TILE,
            bytes_accessed=8 * kept_num * rows * TILE,
            transcendentals=0,
        ),
        name="tile_grads",
    )(*args)


def adam_kernel(dp_size, groups, rows_ref, cols_ref, slot_ref, *refs):
    got = refs[0]
    w_refs = refs[1 : 1 + GROUP]
    m1_ref, m2_ref, m1_out, m2_out, w_out, acc, flat = refs[1 + GROUP :]
    step = pl.program_id(0)

    @pl.when(step == 0)
    def _():
        acc[...] = jnp.zeros_like(acc)
        for d in range(dp_size):
            for q in range(CAP):
                slot = slot_ref[d * CAP + q]

                @pl.when(slot >= 0)
                def _():
                    place = pl.ds(pl.multiple_of(slot * PITCH, 8), TILE)
                    acc[place, :] += got[(d * CAP + q) * TILE : (d * CAP + q + 1) * TILE, :].astype(jnp.float32)

    for j in range(GROUP):
        flat[j * PITCH : j * PITCH + TILE, :] = w_refs[j][...].astype(jnp.float32)

    corr_one = 1.0 - beta_one**STEP
    corr_two = 1.0 - beta_two**STEP
    base = step * GROUP * PITCH

    def body(a, carry):
        lanes = pl.ds(pl.multiple_of(a * TILE, TILE), TILE)
        merged = acc[pl.ds(base + a, GROUP, stride=PITCH), :]
        current = flat[pl.ds(a, GROUP, stride=PITCH), :]
        m1 = beta_one * m1_ref[0, :, lanes] + (1.0 - beta_one) * merged
        m2 = beta_two * m2_ref[0, :, lanes] + (1.0 - beta_two) * merged * merged
        update = m1 / (corr_one * (jnp.sqrt(m2 / corr_two) + eps_adam))
        m1_out[0, :, lanes] = m1
        m2_out[0, :, lanes] = m2
        w_out[0, :, lanes] = (current - learn_rate * update).astype(w_out.dtype)
        return carry

    lax.fori_loop(0, TILE, body, 0, unroll=8)


def adam(rows, cols, slots, got, weight, moment1, moment2):
    dp_size = got.shape[0] // (CAP * TILE)
    _, own_count, flat_size = moment1.shape
    groups = rows.shape[0] // GROUP
    in_specs = [pl.BlockSpec(got.shape, lambda i, r, c, s: (0, 0))]
    for j in range(GROUP):
        in_specs.append(
            pl.BlockSpec(
                (TILE, TILE), lambda i, r, c, s, j=j: (r[i * GROUP + j], c[i * GROUP + j])
            )
        )
    moment_spec = pl.BlockSpec((1, GROUP, flat_size), lambda i, r, c, s: (0, i, 0))
    in_specs += [moment_spec, moment_spec]
    return pl.pallas_call(
        functools.partial(adam_kernel, dp_size, groups),
        out_shape=[
            jax.ShapeDtypeStruct(moment1.shape, jnp.float32),
            jax.ShapeDtypeStruct(moment1.shape, jnp.float32),
            jax.ShapeDtypeStruct(moment1.shape, jnp.bfloat16),
        ],
        grid_spec=pltpu.PrefetchScalarGridSpec(
            num_scalar_prefetch=3,
            grid=(groups,),
            in_specs=in_specs,
            out_specs=[moment_spec, moment_spec, moment_spec],
            scratch_shapes=[
                pltpu.VMEM((groups * GROUP * PITCH, TILE), jnp.float32),
                pltpu.VMEM((GROUP * PITCH, TILE), jnp.float32),
            ],
        ),
        compiler_params=pltpu.CompilerParams(vmem_limit_bytes=24 * 2**20),
        cost_estimate=pl.CostEstimate(
            flops=20 * own_count * flat_size,
            bytes_accessed=20 * own_count * flat_size,
            transcendentals=own_count * flat_size,
        ),
        name="adam",
    )(rows, cols, slots, got, *[weight] * GROUP, moment1, moment2)


def shards(hidden_act, out_grad, down_weight, kept_tiles, tile_owner, moment1, moment2):
    tok_rows = hidden_act.shape[0]
    blk_cols = down_weight.shape[1] // TILE
    own_count = moment1.shape[1]
    dp_size = lax.axis_size("dp")
    tensor_size = lax.axis_size("tensor")
    chips = tensor_size // 2
    me = lax.axis_index("dp").astype(jnp.int32)
    rank = lax.axis_index("tensor").astype(jnp.int32)
    chip, core = rank // 2, rank % 2

    kept = kept_tiles.reshape(-1)
    kept_num = kept.shape[0]
    everyone = kept
    reach = 1
    while reach < dp_size:
        ring = [(i, (i + reach) % dp_size) for i in range(dp_size)]
        more = everyone[: (min(2 * reach, dp_size) - reach) * kept_num]
        everyone = jnp.concatenate([everyone, lax.ppermute(more, "dp", ring)])
        reach *= 2

    swap = [(i, i ^ 1) for i in range(tensor_size)]
    shard = out_grad.shape[0]
    part = shard // CHUNKS
    mine = [out_grad[k * part : (k + 1) * part] for k in range(CHUNKS)]
    far = []
    for hop in range(1, chips):
        ring = [(i, (i + 2 * hop) % tensor_size) for i in range(tensor_size)]
        far.append([lax.ppermute(piece, "tensor", ring) for piece in mine])

    owner = tile_owner.reshape(-1)
    numbers = jnp.arange(owner.shape[0], dtype=jnp.int32)
    before = (owner[:, None] == owner[None, :]) & (numbers[None, :] < numbers[:, None])
    slot_of = jnp.sum(before.astype(jnp.int32), axis=1)
    hit = everyone[:, None] == numbers[None, :]
    kept_owner = jnp.sum(jnp.where(hit, owner[None, :], 0), axis=1).reshape(dp_size, kept_num)
    kept_slot = jnp.sum(jnp.where(hit, slot_of[None, :], 0), axis=1).reshape(dp_size, kept_num)
    order = jnp.arange(kept_num, dtype=jnp.int32)
    same = (kept_owner[:, :, None] == kept_owner[:, None, :]) & (
        order[None, None, :] < order[None, :, None]
    )
    kept_rank = jnp.sum(same.astype(jnp.int32), axis=2)
    place = kept_owner[0] * CAP + kept_rank[0]
    seats = jnp.arange(CAP, dtype=jnp.int32)[None, :, None]
    seated = (kept_owner == me)[:, None, :] & (kept_rank[:, None, :] == seats)
    slots = jnp.sum(jnp.where(seated, kept_slot[:, None, :] + 1, 0), axis=2) - 1
    devices = jnp.arange(dp_size, dtype=jnp.int32)
    source_hit = (me - devices[None, :] + dp_size) % dp_size == devices[:, None]
    slots = jnp.sum(jnp.where(source_hit[:, :, None], slots[None], 0), axis=1).reshape(-1)
    padded = -(-own_count // GROUP) * GROUP
    mask = (owner == me)[None, :] & (
        slot_of[None, :] == jnp.arange(padded, dtype=jnp.int32)[:, None]
    )
    owned = jnp.sum(jnp.where(mask, numbers[None, :], 0), axis=1)

    def block_pos(source, chunk, count):
        side = source * 2
        blocks = [(side + core) * count + chunk, (side + 1 - core) * count + chunk]
        return jnp.concatenate([jnp.stack(blocks), kept % blk_cols, place])

    turned = turned_tiles(kept // blk_cols, hidden_act)
    near = [out_grad, lax.ppermute(out_grad, "tensor", swap)]
    partial = tile_part(
        block_pos(chip, 0, 1), turned, near, None, kept_num, dp_size, chips == 1
    )
    grad_hidden = grad_hidden_part(
        jnp.stack([chip, core]), near, down_weight, tok_rows, None
    )
    for hop, got in enumerate(far, 1):
        source = (chip - hop + chips) % chips
        pieces = []
        for k, piece in enumerate(got):
            if k == CHUNKS - 1:
                piece, partial, grad_hidden, owned, slots = lax.optimization_barrier(
                    (piece, partial, grad_hidden, owned, slots)
                )
            else:
                piece, partial = lax.optimization_barrier((piece, partial))
            pieces.append([piece, lax.ppermute(piece, "tensor", swap)])
            partial = tile_part(
                block_pos(source, k, CHUNKS),
                turned,
                pieces[k],
                partial,
                kept_num,
                dp_size,
                hop == chips - 1 and k == CHUNKS - 1,
            )
        ordered = [pair[0] for pair in pieces] + [pair[1] for pair in pieces]
        grad_hidden = grad_hidden_part(
            jnp.stack([source, core]), ordered, down_weight, tok_rows, grad_hidden
        )

    tiles = lax.all_to_all(partial, "dp", 0, 0, tiled=True)
    moment1_new, moment2_new, weight_tiles = adam(
        owned // blk_cols, owned % blk_cols, slots, tiles, down_weight, moment1, moment2
    )
    return (grad_hidden, moment1_new, moment2_new, weight_tiles)


def solution(mesh):
    in_specs = (
        P("dp", "tensor"),
        P(("dp", "tensor"), None),
        P("tensor", None),
        P("dp", "tensor"),
        P("tensor", None),
        P("dp", "tensor", None),
        P("dp", "tensor", None),
    )
    out_specs = (
        P("dp", "tensor"),
        P("dp", "tensor", None),
        P("dp", "tensor", None),
        P("dp", "tensor", None),
    )
    return jax.shard_map(shards, mesh=mesh, in_specs=in_specs, out_specs=out_specs, check_vma=False)
```

```python
import functools

import jax
import jax.numpy as jnp
from jax import lax
from jax.experimental import pallas as pl
from jax.experimental.pallas import tpu as pltpu
from jax.sharding import PartitionSpec as P

TILE = 128
STEP = 10
CAP = 3
CHUNKS = 1
PITCH = TILE + 8
HID_BLK = 256
GROUP = 8

beta_one = 0.9
beta_two = 0.95
eps_adam = 1e-08
learn_rate = 0.001


def matmul_kernel(num, pos_ref, *refs):
    pieces = refs[: 2 * num]
    w_ref = refs[2 * num]
    out_ref, held = refs[-2], refs[-1]
    rows = pieces[0].shape[0]
    core = pos_ref[1]

    @pl.when(pl.program_id(0) == 0)
    def _():
        for k in range(num):
            mine = pl.multiple_of((core * num + k) * rows, rows)
            held[pl.ds(mine, rows), :] = pieces[k][...]
            other = pl.multiple_of(((1 - core) * num + k) * rows, rows)
            held[pl.ds(other, rows), :] = pieces[num + k][...]

    out_ref[...] = lax.dot_general(
        held[...], w_ref[...], (((1,), (1,)), ((), ())), preferred_element_type=jnp.float32
    ).astype(out_ref.dtype)


def grad_hidden_part(pos, pieces, weight, tok_rows, prev):
    num = len(pieces) // 2
    rows, width = pieces[0].shape
    hid = weight.shape[0]
    pair = 2 * num * rows
    in_specs = [pl.BlockSpec((rows, width), lambda j, s: (0, 0)) for _ in pieces]
    in_specs.append(pl.BlockSpec((HID_BLK, width), lambda j, s: (j, 0)))
    args = [pos, *pieces, weight]
    aliases = {}
    if prev is not None:
        in_specs.append(pl.BlockSpec(memory_space=pl.ANY))
        aliases = {len(args): 0}
        args.append(prev)
    return pl.pallas_call(
        functools.partial(matmul_kernel, num),
        out_shape=jax.ShapeDtypeStruct((tok_rows, hid), jnp.bfloat16),
        grid_spec=pltpu.PrefetchScalarGridSpec(
            num_scalar_prefetch=1,
            grid=(hid // HID_BLK,),
            in_specs=in_specs,
            out_specs=pl.BlockSpec((pair, HID_BLK), lambda j, s: (s[0], j)),
            scratch_shapes=[pltpu.VMEM((pair, width), jnp.bfloat16)],
        ),
        input_output_aliases=aliases,
        compiler_params=pltpu.CompilerParams(vmem_limit_bytes=58 * 2**20),
        cost_estimate=pl.CostEstimate(
            flops=2 * pair * width * hid, bytes_accessed=2 * hid * width, transcendentals=0
        ),
        name="grad_hidden",
    )(*args)


def turn_kernel(pos_ref, h_ref, out_ref):
    out_ref[...] = h_ref[...].T


def turned_tiles(kept_rows, hidden_act):
    kept_num = kept_rows.shape[0]
    tokens = hidden_act.shape[0]
    return pl.pallas_call(
        turn_kernel,
        out_shape=jax.ShapeDtypeStruct((kept_num * TILE, tokens), jnp.bfloat16),
        grid_spec=pltpu.PrefetchScalarGridSpec(
            num_scalar_prefetch=1,
            grid=(kept_num,),
            in_specs=[pl.BlockSpec((tokens, TILE), lambda p, s: (0, s[p]))],
            out_specs=pl.BlockSpec((TILE, tokens), lambda p, s: (p, 0)),
        ),
        compiler_params=pltpu.CompilerParams(vmem_limit_bytes=8 * 2**20),
        cost_estimate=pl.CostEstimate(
            flops=0, bytes_accessed=16 * kept_num * tokens * TILE, transcendentals=0
        ),
        name="turned_tiles",
    )(kept_rows, hidden_act)


def tile_kernel(kept_num, has_prev, last, pos_ref, h_ref, g_mine, g_other, *refs):
    rows = g_mine.shape[0]
    mine = pl.ds(pl.multiple_of(pos_ref[0] * rows, rows), rows)
    other = pl.ds(pl.multiple_of(pos_ref[1] * rows, rows), rows)
    pack = refs[-1]
    if last:
        pack[...] = jnp.zeros_like(pack)
    for p in range(kept_num):
        tile = pl.ds(p * TILE, TILE)
        lanes = pl.ds(pl.multiple_of(pos_ref[2 + p] * TILE, TILE), TILE)
        total = jnp.dot(h_ref[tile, mine], g_mine[:, lanes], preferred_element_type=jnp.float32)
        total += jnp.dot(h_ref[tile, other], g_other[:, lanes], preferred_element_type=jnp.float32)
        if has_prev:
            total = total + refs[0][tile, :]
        if last:
            place = pl.multiple_of(pos_ref[2 + kept_num + p] * TILE, TILE)
            pack[pl.ds(place, TILE), :] = total.astype(pack.dtype)
        else:
            refs[-1][tile, :] = total


def tile_part(pos, turned, pieces, prev, kept_num, dp_size, last):
    rows = pieces[0].shape[0]
    args = [pos, turned, *pieces]
    if prev is not None:
        args.append(prev)
    if last:
        out_shape = jax.ShapeDtypeStruct((dp_size * CAP * TILE, TILE), jnp.bfloat16)
    else:
        out_shape = jax.ShapeDtypeStruct((kept_num * TILE, TILE), jnp.float32)
    whole = pl.BlockSpec(memory_space=pltpu.VMEM)
    return pl.pallas_call(
        functools.partial(tile_kernel, kept_num, prev is not None, last),
        out_shape=out_shape,
        in_specs=[pl.BlockSpec(memory_space=pltpu.SMEM)] + [whole] * (len(args) - 1),
        out_specs=whole,
        compiler_params=pltpu.CompilerParams(vmem_limit_bytes=24 * 2**20),
        cost_estimate=pl.CostEstimate(
            flops=4 * kept_num * rows * TILE * TILE,
            bytes_accessed=8 * kept_num * rows * TILE,
            transcendentals=0,
        ),
        name="tile_grads",
    )(*args)


def adam_kernel(dp_size, groups, rows_ref, cols_ref, slot_ref, *refs):
    got = refs[0]
    w_refs = refs[1 : 1 + GROUP]
    m1_ref, m2_ref, m1_out, m2_out, w_out, acc, flat = refs[1 + GROUP :]
    step = pl.program_id(0)

    @pl.when(step == 0)
    def _():
        acc[...] = jnp.zeros_like(acc)
        for d in range(dp_size):
            for q in range(CAP):
                slot = slot_ref[d * CAP + q]

                @pl.when(slot >= 0)
                def _():
                    place = pl.ds(pl.multiple_of(slot * PITCH, 8), TILE)
                    acc[place, :] += got[(d * CAP + q) * TILE : (d * CAP + q + 1) * TILE, :].astype(jnp.float32)

    for j in range(GROUP):
        flat[j * PITCH : j * PITCH + TILE, :] = w_refs[j][...].astype(jnp.float32)

    corr_one = 1.0 - beta_one**STEP
    corr_two = 1.0 - beta_two**STEP
    base = step * GROUP * PITCH

    def body(a, carry):
        lanes = pl.ds(pl.multiple_of(a * TILE, TILE), TILE)
        merged = acc[pl.ds(base + a, GROUP, stride=PITCH), :]
        current = flat[pl.ds(a, GROUP, stride=PITCH), :]
        m1 = beta_one * m1_ref[0, :, lanes] + (1.0 - beta_one) * merged
        m2 = beta_two * m2_ref[0, :, lanes] + (1.0 - beta_two) * merged * merged
        update = m1 / (corr_one * (jnp.sqrt(m2 / corr_two) + eps_adam))
        m1_out[0, :, lanes] = m1
        m2_out[0, :, lanes] = m2
        w_out[0, :, lanes] = (current - learn_rate * update).astype(w_out.dtype)
        return carry

    lax.fori_loop(0, TILE, body, 0, unroll=8)


def adam(rows, cols, slots, got, weight, moment1, moment2):
    dp_size = got.shape[0] // (CAP * TILE)
    _, own_count, flat_size = moment1.shape
    groups = rows.shape[0] // GROUP
    in_specs = [pl.BlockSpec(got.shape, lambda i, r, c, s: (0, 0))]
    for j in range(GROUP):
        in_specs.append(
            pl.BlockSpec(
                (TILE, TILE), lambda i, r, c, s, j=j: (r[i * GROUP + j], c[i * GROUP + j])
            )
        )
    moment_spec = pl.BlockSpec((1, GROUP, flat_size), lambda i, r, c, s: (0, i, 0))
    in_specs += [moment_spec, moment_spec]
    return pl.pallas_call(
        functools.partial(adam_kernel, dp_size, groups),
        out_shape=[
            jax.ShapeDtypeStruct(moment1.shape, jnp.float32),
            jax.ShapeDtypeStruct(moment1.shape, jnp.float32),
            jax.ShapeDtypeStruct(moment1.shape, jnp.bfloat16),
        ],
        grid_spec=pltpu.PrefetchScalarGridSpec(
            num_scalar_prefetch=3,
            grid=(groups,),
            in_specs=in_specs,
            out_specs=[moment_spec, moment_spec, moment_spec],
            scratch_shapes=[
                pltpu.VMEM((groups * GROUP * PITCH, TILE), jnp.float32),
                pltpu.VMEM((GROUP * PITCH, TILE), jnp.float32),
            ],
        ),
        compiler_params=pltpu.CompilerParams(vmem_limit_bytes=58 * 2**20),
        cost_estimate=pl.CostEstimate(
            flops=20 * own_count * flat_size,
            bytes_accessed=20 * own_count * flat_size,
            transcendentals=own_count * flat_size,
        ),
        name="adam",
    )(rows, cols, slots, got, *[weight] * GROUP, moment1, moment2)


def shards(hidden_act, out_grad, down_weight, kept_tiles, tile_owner, moment1, moment2):
    tok_rows = hidden_act.shape[0]
    blk_cols = down_weight.shape[1] // TILE
    own_count = moment1.shape[1]
    dp_size = lax.axis_size("dp")
    tensor_size = lax.axis_size("tensor")
    chips = tensor_size // 2
    me = lax.axis_index("dp").astype(jnp.int32)
    rank = lax.axis_index("tensor").astype(jnp.int32)
    chip, core = rank // 2, rank % 2

    kept = kept_tiles.reshape(-1)
    kept_num = kept.shape[0]
    everyone = kept
    reach = 1
    while reach < dp_size:
        ring = [(i, (i + reach) % dp_size) for i in range(dp_size)]
        more = everyone[: (min(2 * reach, dp_size) - reach) * kept_num]
        everyone = jnp.concatenate([everyone, lax.ppermute(more, "dp", ring)])
        reach *= 2

    swap = [(i, i ^ 1) for i in range(tensor_size)]
    shard = out_grad.shape[0]
    part = shard // CHUNKS
    mine = [out_grad[k * part : (k + 1) * part] for k in range(CHUNKS)]
    far = []
    for hop in range(1, chips):
        ring = [(i, (i + 2 * hop) % tensor_size) for i in range(tensor_size)]
        far.append([lax.ppermute(piece, "tensor", ring) for piece in mine])

    owner = tile_owner.reshape(-1)
    numbers = jnp.arange(owner.shape[0], dtype=jnp.int32)
    before = (owner[:, None] == owner[None, :]) & (numbers[None, :] < numbers[:, None])
    slot_of = jnp.sum(before.astype(jnp.int32), axis=1)
    hit = everyone[:, None] == numbers[None, :]
    kept_owner = jnp.sum(jnp.where(hit, owner[None, :], 0), axis=1).reshape(dp_size, kept_num)
    kept_slot = jnp.sum(jnp.where(hit, slot_of[None, :], 0), axis=1).reshape(dp_size, kept_num)
    order = jnp.arange(kept_num, dtype=jnp.int32)
    same = (kept_owner[:, :, None] == kept_owner[:, None, :]) & (
        order[None, None, :] < order[None, :, None]
    )
    kept_rank = jnp.sum(same.astype(jnp.int32), axis=2)
    place = kept_owner[0] * CAP + kept_rank[0]
    seats = jnp.arange(CAP, dtype=jnp.int32)[None, :, None]
    seated = (kept_owner == me)[:, None, :] & (kept_rank[:, None, :] == seats)
    slots = jnp.sum(jnp.where(seated, kept_slot[:, None, :] + 1, 0), axis=2) - 1
    devices = jnp.arange(dp_size, dtype=jnp.int32)
    source_hit = (me - devices[None, :] + dp_size) % dp_size == devices[:, None]
    slots = jnp.sum(jnp.where(source_hit[:, :, None], slots[None], 0), axis=1).reshape(-1)
    padded = -(-own_count // GROUP) * GROUP
    mask = (owner == me)[None, :] & (
        slot_of[None, :] == jnp.arange(padded, dtype=jnp.int32)[:, None]
    )
    owned = jnp.sum(jnp.where(mask, numbers[None, :], 0), axis=1)

    def block_pos(source, chunk, count):
        side = source * 2
        blocks = [(side + core) * count + chunk, (side + 1 - core) * count + chunk]
        return jnp.concatenate([jnp.stack(blocks), kept % blk_cols, place])

    turned = turned_tiles(kept // blk_cols, hidden_act)
    near = [out_grad, lax.ppermute(out_grad, "tensor", swap)]
    partial = tile_part(
        block_pos(chip, 0, 1), turned, near, None, kept_num, dp_size, chips == 1
    )
    grad_hidden = grad_hidden_part(
        jnp.stack([chip, core]), near, down_weight, tok_rows, None
    )
    for hop, got in enumerate(far, 1):
        source = (chip - hop + chips) % chips
        pieces = []
        for k, piece in enumerate(got):
            if k == CHUNKS - 1:
                piece, partial, grad_hidden, owned, slots = lax.optimization_barrier(
                    (piece, partial, grad_hidden, owned, slots)
                )
            else:
                piece, partial = lax.optimization_barrier((piece, partial))
            pieces.append([piece, lax.ppermute(piece, "tensor", swap)])
            partial = tile_part(
                block_pos(source, k, CHUNKS),
                turned,
                pieces[k],
                partial,
                kept_num,
                dp_size,
                hop == chips - 1 and k == CHUNKS - 1,
            )
        ordered = [pair[0] for pair in pieces] + [pair[1] for pair in pieces]
        grad_hidden = grad_hidden_part(
            jnp.stack([source, core]), ordered, down_weight, tok_rows, grad_hidden
        )

    tiles = lax.all_to_all(partial, "dp", 0, 0, tiled=True)
    moment1_new, moment2_new, weight_tiles = adam(
        owned // blk_cols, owned % blk_cols, slots, tiles, down_weight, moment1, moment2
    )
    return (grad_hidden, moment1_new, moment2_new, weight_tiles)


def solution(mesh):
    in_specs = (
        P("dp", "tensor"),
        P(("dp", "tensor"), None),
        P("tensor", None),
        P("dp", "tensor"),
        P("tensor", None),
        P("dp", "tensor", None),
        P("dp", "tensor", None),
    )
    out_specs = (
        P("dp", "tensor"),
        P("dp", "tensor", None),
        P("dp", "tensor", None),
        P("dp", "tensor", None),
    )
    return jax.shard_map(shards, mesh=mesh, in_specs=in_specs, out_specs=out_specs, check_vma=False)
```
